256 devices in a mesh: ctx: 8 (over x, y_lo), mp: 32 (over z, y_hi, core).
Axes of the slice: x: 4, y: 4 (y_hi: 2, y_lo: 2; y = y_hi * 2 + y_lo), z: 8, core: 2. Of those that a mesh axis runs over, the one named last changes fastest.
Arguments:
- residual_in: bfloat16 [4096, 8192], P('ctx', 'mp'), may hold values from -4 to 4
- query_rows: bfloat16 [4096, 8192], P('ctx', 'mp'), may hold values from -5 to 5
- key_rows: bfloat16 [4096, 8192], P('ctx', 'mp'), may hold values from -5 to 5
- value_rows: bfloat16 [4096, 8192], P('ctx', 'mp'), may hold values from -5 to 5
- out_weight: bfloat16 [8192, 8192], P('mp'), may hold values from -1 to 1
- gate_in: bfloat16 [4096, 8192], P('ctx', 'mp'), may hold values from -5 to 5
- gate_out: bfloat16 [4096, 8192], P('ctx', 'mp'), may hold values from -5 to 5
- short_taps: float32 [3, 8192], P(None, 'mp'), may hold values from -3 to 3
- decay_rates: float32 [16, 8192], P(None, 'mp'), may hold values from 4.8828126e-05 to 0.03
- residues: float32 [16, 8192], P(None, 'mp'), may hold values from -0.15 to 0.15
- skip_gain: float32 [8192], P('mp'), may hold values from -4 to 4
Outputs:
- attended: bfloat16 [4096, 8192], P('ctx', 'mp')
- hyena_out: bfloat16 [4096, 8192], P('ctx', 'mp')
The draws below stay inside these ranges and needn't reach their ends.
All inputs are finite; a program needn't handle non-finite values.
Results may differ from the reference program's by a relative error of at most 0.02.
Values may be sent and summed in bfloat16 or wider, within the bound.
No kernel may reach another device: no remote copies, remote signals or barrier semaphores. Data moves between devices by JAX's collectives and lax.ppermute only.
A program may use at most 128 MiB of HBM per device.

```python
import math
import jax
import jax.numpy as jnp
from jax import lax

D = 8192
HEADS = 64
HD = 128
POLES = 16
TAPS = 3
BLOCK = 64
SEQ = 4096
N_MP = 32


def drawn_rows(key, salt):
    sub = jax.random.fold_in(key, salt)
    return jnp.clip(jax.random.normal(sub, (SEQ, HEADS * HD), jnp.float32), -5.0, 5.0)


def draw_query_rows(key, part):
    drawn = drawn_rows(key, 1)
    return drawn.astype(jnp.bfloat16)


def draw_key_rows(key, part):
    drawn = drawn_rows(key, 2)
    return drawn.astype(jnp.bfloat16)


def with_spikes(values, own_key, source, target, blocks, factor):
    def block_of(dim):
        return (jnp.arange(values.shape[dim]) // (values.shape[dim] // blocks)).reshape((-1,) + (1,) * (values.ndim - 1 - dim))

    one_side = jax.random.permutation(own_key, blocks)[block_of(target)]
    second = (block_of(target) + blocks // 2) % blocks
    return jnp.where((block_of(source) == one_side) | (block_of(source) == second), factor * values, values)


def level_of(own_key, extent, shards, smallest, high):
    loudness = 1.0
    for dim, blocks in shards:
        heights = jax.random.uniform(jax.random.fold_in(jax.random.fold_in(own_key, 6), dim), (blocks,), jnp.float32, smallest / len(shards), high / len(shards))
        loudness = loudness * jnp.repeat(jnp.exp(heights), extent[dim] // blocks).reshape((-1,) + (1,) * (len(extent) - 1 - dim))
    return loudness


def normal_values(own_key, dims, scale, bound, cuts=(), held_as=jnp.bfloat16):
    loudness = level_of(own_key, dims, cuts, -0.22, 0.18) if cuts else 1.0
    drawn = jax.random.normal(own_key, dims, jnp.float32) * scale * loudness
    return jnp.minimum(jnp.maximum(drawn, -bound), bound).astype(held_as)


def heavy_noise(rng, dims, spread, bound, split, heavy, kind=jnp.bfloat16):
    values = spread * jax.random.normal(rng, dims, jnp.float32)
    if split:
        values = values * level_of(rng, dims, split, -0.22, 0.18)
    return jnp.clip(with_spikes(values, jax.random.fold_in(rng, 3), *heavy), -bound, bound).astype(kind)


def setup_inputs(seed: int = 0) -> dict:
    key_of = jax.random.split(jax.random.key(seed), 12)
    residual_in = normal_values(key_of[0], (SEQ, D), 0.5, 4.0, ((0, 8), (1, 32)))
    query_rows = draw_query_rows(jax.random.fold_in(key_of[11], 71), 0)
    key_rows = draw_key_rows(jax.random.fold_in(key_of[11], 71), 0)
    value_rows = normal_values(key_of[3], (SEQ, HEADS * HD), 1.0, 5.0, ((0, 8), (1, 32)))
    out_weight = heavy_noise(key_of[4], (HEADS * HD, D), HD ** -0.5, 1.0, ((0, 32),), (0, 1, 32, 2.75))
    gate_in = normal_values(key_of[5], (SEQ, D), 1.0, 5.0, ((0, 8), (1, 32)))
    gate_out = normal_values(key_of[6], (SEQ, D), 1.0, 5.0, ((0, 8), (1, 32)))
    short_taps = normal_values(key_of[7], (TAPS, D), 0.6, 3.0, ((1, 32),), jnp.float32)
    decay_rates = jnp.clip(jnp.exp(math.log(0.03) - 6.420646 * jax.random.uniform(key_of[8], (POLES, D), jnp.float32) ** level_of(key_of[8], (POLES, D), ((1, 32),), -0.2, 0.2)), 4.882812572759576e-05, 0.03)
    residues = normal_values(key_of[9], (POLES, D), 0.03, 0.15, ((1, 32),), jnp.float32)
    skip_gain = normal_values(key_of[10], (D,), 1.0, 4.0, ((0, 32),), jnp.float32)
    return {"residual_in": residual_in, "query_rows": query_rows, "key_rows": key_rows, "value_rows": value_rows, "out_weight": out_weight, "gate_in": gate_in, "gate_out": gate_out, "short_taps": short_taps, "decay_rates": decay_rates, "residues": residues, "skip_gain": skip_gain}


masked_floor = -1e30


def head_attention(query_head, key_head, value_head):
    scores = jnp.dot(query_head, key_head.T, preferred_element_type=jnp.float32) * (HD ** -0.5)
    positions = jnp.arange(SEQ)
    allowed = positions[None, :] <= positions[:, None]
    masked = jnp.where(allowed, scores, masked_floor)
    highest = jnp.max(masked, axis=1, keepdims=True)
    weights = jnp.where(allowed, jnp.exp(masked - highest), 0.0)
    total = jnp.sum(weights, axis=1, keepdims=True)
    summed = jnp.dot(weights.astype(jnp.bfloat16), value_head, preferred_element_type=jnp.float32)
    return summed / total


def modal_tables(decay_rates, residues, block):
    width = decay_rates.shape[1]
    lags = jnp.arange(block).astype(jnp.float32)
    lag_diff = lags[:, None] - lags[None, :]
    causal = lag_diff >= 0
    safe_diff = jnp.maximum(lag_diff, 0.0)

    def add_pole(total, pole):
        rate, residue = pole
        return total + residue[None, None, :] * jnp.exp(-rate[None, None, :] * safe_diff[:, :, None]), None

    toeplitz, _ = lax.scan(add_pole, jnp.zeros((block, block, width), jnp.float32), (decay_rates, residues))
    toeplitz = jnp.where(causal[:, :, None], toeplitz, 0.0)
    powers = jnp.exp(-decay_rates[None] * lags[:, None, None])
    inward = jnp.exp(-decay_rates[None] * (block - lags)[:, None, None])
    return toeplitz, powers, inward


def modal_conv(signal, decay_rates, residues, block):
    length, width = signal.shape
    toeplitz, powers, inward = modal_tables(decay_rates, residues, block)
    highest = lax.Precision.HIGHEST
    span = jnp.exp(-decay_rates * block)

    def step(state, piece):
        local = jnp.einsum('ijc,jc->ic', toeplitz, piece, precision=highest)
        carried = jnp.einsum('inc,nc->ic', powers, residues * state, precision=highest)
        state = span * state + jnp.einsum('jnc,jc->nc', inward, piece, precision=highest)
        return state, local + carried

    start_state = jnp.zeros((decay_rates.shape[0], width), jnp.float32)
    state, result = lax.scan(step, start_state, signal.reshape(length // block, block, width))
    return result.reshape(length, width), state


def reference(residual_in, query_rows, key_rows, value_rows, out_weight, gate_in, gate_out, short_taps, decay_rates, residues, skip_gain):
    def by_head(arr):
        return arr.reshape(SEQ, HEADS, HD).transpose(1, 0, 2)

    heads_out = lax.map(lambda trio: head_attention(trio[0], trio[1], trio[2]), (by_head(query_rows), by_head(key_rows), by_head(value_rows)))
    heads_out = heads_out.transpose(1, 0, 2).reshape(SEQ, HEADS * HD).astype(jnp.bfloat16)
    group_cols = HEADS * HD // N_MP
    head_groups = heads_out.reshape(SEQ, N_MP, group_cols).transpose(1, 0, 2)
    weight_groups = out_weight.reshape(N_MP, group_cols, D)

    def add_group(total, pair):
        partial_sum = jnp.dot(pair[0], pair[1], preferred_element_type=jnp.float32)
        rounded = lax.optimization_barrier(partial_sum.astype(jnp.bfloat16))
        return total + rounded.astype(jnp.float32), None

    projected, _ = lax.scan(add_group, jnp.zeros((SEQ, D), jnp.float32), (head_groups, weight_groups))
    attended = (residual_in.astype(jnp.float32) + projected).astype(jnp.bfloat16)
    stream = attended.astype(jnp.float32)
    padded = jnp.concatenate([jnp.zeros((TAPS - 1, D), jnp.float32), stream], axis=0)
    shortconv = jnp.zeros((SEQ, D), jnp.float32)
    for tap in range(TAPS):
        shortconv = shortconv + short_taps[tap][None, :] * padded[TAPS - 1 - tap:TAPS - 1 - tap + SEQ]
    signal = gate_in.astype(jnp.float32) * shortconv
    longconv, _ = modal_conv(signal, decay_rates, residues, BLOCK)
    hyena_out = (gate_out.astype(jnp.float32) * (longconv + skip_gain[None, :] * signal)).astype(jnp.bfloat16)
    return attended, hyena_out
```

```python
import jax
import jax.numpy as jnp
from jax import lax
from jax.experimental import pallas as pl
from jax.experimental.pallas import tpu as pltpu
from jax.sharding import Mesh
from jax.sharding import PartitionSpec as P

HD = 128
BLOCK = 64
NX, NYL, NZ, NYH, NC = (4, 2, 8, 2, 2)
masked_floor = -1e30
LOG2E = 1.4426950408889634
VM = 60 * 1024 * 1024


def vmem_params(**kw):
    return pltpu.CompilerParams(vmem_limit_bytes=VM, **kw)


def struct(shape, dtype):
    return jax.ShapeDtypeStruct(shape, dtype)


def dot(a, b):
    return jnp.dot(a, b, preferred_element_type=jnp.float32)


def pack_kernel(q_ref, k_ref, v_ref, *outs):
    t_refs, q_refs = (outs[:4], outs[4:])
    half = q_ref.shape[0] // 2
    x = lax.axis_index("x")
    for a in range(4):
        head = (x & 1) ^ (a & 1)
        core = (x >> 1) ^ (a >> 1)
        cols = pl.ds(pl.multiple_of(head * HD, HD), HD)

        @pl.when(core == 0)
        def _(a=a, cols=cols):
            t_refs[a][...] = k_ref[:, cols]

        @pl.when(core == 1)
        def _(a=a, cols=cols):
            t_refs[a][...] = v_ref[:, cols]

        rows = pl.ds(pl.multiple_of(core * half, half), half)
        q_refs[a][...] = q_ref[rows, cols]


def head_route(a):
    pairs = []
    for x in range(NX):
        for c in range(NC):
            to_x = 2 * c + ((x & 1) ^ (a & 1))
            to_c = (x >> 1) ^ (a >> 1)
            pairs.append((x * NC + c, to_x * NC + to_c))
    return pairs


def attend_kernel(q0, q1, q2, q3, own_m, own_x, far_m, far_x, *rest):
    outs = rest[:4]
    q_s, k_s, v_s, s_s = rest[4:]
    x = lax.axis_index("x")
    yl = lax.axis_index("yl")
    c = lax.axis_index("c")
    x0 = x & 1
    rows = q0.shape[0]
    keys = own_m.shape[1]
    for a, ref in enumerate((q0, q1, q2, q3)):
        q_s[2 * (c ^ (a >> 1)) + (x0 ^ (a & 1))] = ref[...]

    def order(k_src, v_src, segment):
        for xs in range(4):
            low = x0 ^ (xs & 1)
            slot = 2 * xs + segment
            k_s[slot] = k_src[2 * (xs >> 1) + low]
            v_s[slot] = v_src[2 * (1 ^ (xs >> 1)) + low]

    @pl.when(c == 0)
    def _():
        order(own_m, own_x, yl)
        order(far_m, far_x, 1 - yl)

    @pl.when(c == 1)
    def _():
        order(own_x, own_m, yl)
        order(far_x, far_m, 1 - yl)

    factor = HD ** (-0.5) * LOG2E

    def lanes(op, wide):
        parts = [wide[:, i * HD : (i + 1) * HD] for i in range(keys // HD)]
        while len(parts) > 1:
            parts = [op(parts[i], parts[i + 1]) for i in range(0, len(parts), 2)]
        return parts[0]

    for d in range(4):
        xs = (x + d) & 3
        last = 2 * xs + yl
        query = q_s[xs]

        def scores_of(s, query=query):
            return lax.dot_general(
                query, k_s[s], (((1,), (1,)), ((), ())), preferred_element_type=jnp.float32
            )

        def first(s, top, scores_of=scores_of):
            sc = scores_of(s)
            s_s[s] = sc
            return jnp.maximum(top, lanes(jnp.maximum, sc))

        sc = scores_of(last)
        row = lax.broadcasted_iota(jnp.int32, (rows, keys), 0) + c * rows
        col = lax.broadcasted_iota(jnp.int32, (rows, keys), 1)
        sc = jnp.where(col <= row, sc, masked_floor)
        s_s[last] = sc
        top = lax.fori_loop(0, last, first, lanes(jnp.maximum, sc))
        top = jnp.max(top, axis=1, keepdims=True)

        def second(s, carry, top=top):
            total, acc = carry
            p = jnp.exp2((s_s[s] - top) * factor)
            return (total + lanes(jnp.add, p), acc + dot(p.astype(jnp.bfloat16), v_s[s]))

        zero = jnp.zeros((rows, HD), jnp.float32)
        total, acc = lax.fori_loop(0, last + 1, second, (zero, zero))
        total = jnp.sum(total, axis=1, keepdims=True)
        outs[d][...] = (acc / total).astype(jnp.bfloat16)


def weight_pick_kernel(meta, w_ref, o_ref):
    o_ref[...] = w_ref[...]


def project_kernel(meta, hm, ho, w_o, w_m, r_o, r_m, out_o, out_m, h_s):
    half = hm.shape[1]
    x = meta[0]
    c = meta[4]

    @pl.when(pl.program_id(0) == 0)
    def _():
        for group in range(2):
            core = c ^ group
            for j in range(2):
                d = (x - 2 * core - j) & 3
                cols = slice(j * HD, (j + 1) * HD)
                h_s[group, pl.ds(pl.multiple_of(c * half, half), half), cols] = hm[d]
                h_s[group, pl.ds(pl.multiple_of((1 - c) * half, half), half), cols] = ho[d]

    out_o[0] = (dot(h_s[0], w_o[...]) + dot(h_s[1], r_o[...])).astype(jnp.bfloat16)
    out_m[0] = (dot(h_s[0], w_m[...]) + dot(h_s[1], r_m[...])).astype(jnp.bfloat16)


def project(meta, hm, ho, weight, w_recv, offsets):
    n = len(offsets)
    k, wide = weight.shape
    width = wide // (NZ * NYH * NC)
    rows = 2 * hm.shape[1]
    start, step = offsets[0], (offsets[1] - offsets[0] if n > 1 else 0)

    def target(i, meta):
        return (meta[2] + start + step * i) & (NZ - 1)

    def whole(shape):
        return pl.BlockSpec(shape, lambda i, meta: (0,) * len(shape))

    specs = [
        whole(hm.shape),
        whole(ho.shape),
        pl.BlockSpec((k, width), lambda i, m: (0, (target(i, m) * NYH + 1 - m[3]) * NC + m[4])),
        pl.BlockSpec((k, width), lambda i, m: (0, (target(i, m) * NYH + m[3]) * NC + m[4])),
        pl.BlockSpec((k, width), lambda i, m: (0, target(i, m) * NYH + 1 - m[3])),
        pl.BlockSpec((k, width), lambda i, m: (0, target(i, m) * NYH + m[3])),
    ]
    out = pl.BlockSpec((1, rows, width), lambda i, m: (i, 0, 0))
    return pl.pallas_call(
        project_kernel,
        out_shape=[struct((n, rows, width), jnp.bfloat16)] * 2,
        grid_spec=pltpu.PrefetchScalarGridSpec(
            num_scalar_prefetch=1,
            grid=(n,),
            in_specs=specs,
            out_specs=[out, out],
            scratch_shapes=[pltpu.VMEM((2, rows, k), jnp.bfloat16)],
        ),
        compiler_params=vmem_params(),
    )(meta, hm, ho, weight, weight, w_recv, w_recv)


def tables_kernel(rate_ref, res_ref, out_t, in_t, filt):
    poles, width = rate_ref.shape
    lag = lax.broadcasted_iota(jnp.int32, (BLOCK, width), 0).astype(jnp.float32)
    total = jnp.zeros((BLOCK, width), jnp.float32)
    for n in range(poles):
        rate = rate_ref[n : n + 1, :]
        piece = res_ref[n : n + 1, :] * jnp.exp(-rate * lag)
        out_t[n] = piece
        in_t[n] = jnp.exp(-rate * (BLOCK - lag))
        total = total + piece
    filt[...] = total


def signal_kernel(own, plus, minus, side, res, gate, taps, rate, in_t, att, sig, blocks, pkg, pad):
    rows, width = res.shape
    poles = rate.shape[0]
    f32 = jnp.float32
    total = (
        own[...].astype(f32) + plus[...].astype(f32) + minus[...].astype(f32) + side[...].astype(f32)
    )
    done = (res[...].astype(f32) + total).astype(jnp.bfloat16)
    att[...] = done
    pad[0:8, :] = jnp.zeros((8, width), f32)
    pad[8 : 8 + rows, :] = done.astype(f32)
    short = (
        taps[0:1, :] * pad[8 : 8 + rows, :]
        + taps[1:2, :] * pad[7 : 7 + rows, :]
        + taps[2:3, :] * pad[6 : 6 + rows, :]
    )
    sig[...] = gate[...].astype(f32) * short
    span = jnp.exp(-rate[...] * BLOCK)

    def step(b, state):
        blocks[b] = state
        piece = sig[pl.ds(pl.multiple_of(b * BLOCK, BLOCK), BLOCK), :]
        sums = [jnp.sum(in_t[n] * piece, axis=0, keepdims=True) for n in range(poles)]
        return span * state + jnp.concatenate(sums, axis=0)

    state = lax.fori_loop(0, rows // BLOCK, step, jnp.zeros((poles, width), f32))
    pkg[0:poles, :] = state
    pkg[poles : poles + 2, :] = pad[6 + rows : 8 + rows, :]
    pkg[poles + 2 : poles + 4, :] = gate[0:2, :].astype(f32)
    pkg[poles + 4 :, :] = jnp.zeros((pkg.shape[0] - poles - 4, width), f32)


def local_kernel(sig, filt, skip, out, pad):
    rows, width = sig.shape
    pad[0:BLOCK, :] = jnp.zeros((BLOCK, width), jnp.float32)

    def step(b, carry):
        at = pl.ds(pl.multiple_of(b * BLOCK, BLOCK), BLOCK)
        piece = sig[at, :]
        pad[BLOCK : 2 * BLOCK, :] = piece
        for lane in range(width // HD):
            cols = slice(lane * HD, (lane + 1) * HD)
            total = (skip[0:1, cols] + filt[0:1, cols]) * piece[:, cols]
            for k in range(1, BLOCK):
                total = total + filt[k : k + 1, cols] * pad[BLOCK - k : 2 * BLOCK - k, cols]
            out[at, cols] = total
        return carry

    lax.fori_loop(0, rows // BLOCK, step, 0)


def finish_kernel(
    local, blocks, g0, g1, g2, g3, out_t, rate_ref, res_ref, taps, skip, gate, out, pk, st
):
    rows, width = local.shape
    poles = rate_ref.shape[0]
    f32 = jnp.float32
    x = lax.axis_index("x")
    yl = lax.axis_index("yl")
    here = 2 * x + yl
    for d, ref in enumerate((g0, g1, g2, g3)):
        pk[d] = ref[...]
    rate = rate_ref[...]
    segment_decay = jnp.exp(-rate * rows)
    almost_decay = jnp.exp(-rate * (rows - 1))
    t1, t2 = (taps[1:2, :], taps[2:3, :])

    def first_two(package, rim):
        d0 = package[poles + 2 : poles + 3, :] * (t1 * rim[1:2, :] + t2 * rim[0:1, :])
        d1 = package[poles + 3 : poles + 4, :] * (t2 * rim[1:2, :])
        return (d0, d1)

    state = jnp.zeros((poles, width), f32)
    rim = jnp.zeros((2, width), f32)
    for s in range(NX * NYL - 1):
        package = pk[(x - (s >> 1)) & 3, (s & 1) ^ yl]
        d0, d1 = first_two(package, rim)
        full = package[0:poles, :] + segment_decay * d0 + almost_decay * d1
        live = s < here
        state = jnp.where(live, state * segment_decay + full, state)
        rim = jnp.where(live, package[poles : poles + 2, :], rim)
    d0, d1 = first_two(pk[0, 0], rim)
    grow = jnp.exp(rate)
    start = state + d0 + d1 * grow
    before = jnp.sum(res_ref[...] * grow, axis=0, keepdims=True)
    for b in range(rows // BLOCK):
        st[b] = blocks[b] + start * jnp.exp(-rate * (b * BLOCK))
    row = lax.broadcasted_iota(jnp.int32, (BLOCK, width), 0)
    extra = jnp.where(row == 0, skip[...] * d0 - before * d1, 0.0)
    extra = extra + jnp.where(row == 1, skip[...] * d1, 0.0)

    def step(b, carry):
        at = pl.ds(pl.multiple_of(b * BLOCK, BLOCK), BLOCK)
        states = st[b]
        total = local[at, :] + jnp.where(b == 0, extra, 0.0)
        for n in range(poles):
            total = total + out_t[n] * states[n : n + 1, :]
        out[at, :] = (gate[at, :].astype(f32) * total).astype(jnp.bfloat16)
        return carry

    lax.fori_loop(0, rows // BLOCK, step, 0)


def shift(value, axis, count, by):
    return lax.ppermute(value, axis, [(i, (i + by) % count) for i in range(count)])


def per_device(
    residual_in,
    query_rows,
    key_rows,
    value_rows,
    out_weight,
    gate_in,
    gate_out,
    short_taps,
    decay_rates,
    residues,
    skip_gain,
):
    rows, width = residual_in.shape
    half = rows // 2
    bf16, f32 = (jnp.bfloat16, jnp.float32)
    poles = decay_rates.shape[0]
    skip = skip_gain.reshape(1, width)

    packed = pl.pallas_call(
        pack_kernel,
        out_shape=[struct((rows, HD), bf16)] * 4 + [struct((half, HD), bf16)] * 4,
        compiler_params=vmem_params(),
    )(query_rows, key_rows, value_rows)
    tensors = [lax.ppermute(packed[a], ("x", "c"), head_route(a)) for a in range(4)]
    queries = [lax.ppermute(packed[4 + a], ("x", "c"), head_route(a)) for a in range(4)]

    meta = jnp.stack([lax.axis_index(name) for name in ("x", "yl", "z", "yh", "c")]).astype(
        jnp.int32
    )
    k_rows, wide = out_weight.shape
    n_cols = NZ * NYH
    w_send = pl.pallas_call(
        weight_pick_kernel,
        out_shape=struct((k_rows, n_cols * width), bf16),
        grid_spec=pltpu.PrefetchScalarGridSpec(
            num_scalar_prefetch=1,
            grid=(n_cols,),
            in_specs=[pl.BlockSpec((k_rows, width), lambda i, m: (0, NC * i + 1 - m[4]))],
            out_specs=pl.BlockSpec((k_rows, width), lambda i, m: (0, i)),
        ),
        compiler_params=vmem_params(),
    )(meta, out_weight)
    w_recv = shift(w_send, "c", NC, 1)
    out_t, in_t, filt = pl.pallas_call(
        tables_kernel,
        out_shape=[struct((poles, BLOCK, width), f32)] * 2 + [struct((BLOCK, width), f32)],
        compiler_params=vmem_params(),
    )(decay_rates, residues)

    own_m = jnp.stack(tensors)
    far_m = shift(own_m, "yl", NYL, 1)
    own_x = shift(own_m, "c", NC, 1)
    far_x = shift(far_m, "c", NC, 1)
    heads = pl.pallas_call(
        attend_kernel,
        out_shape=[struct((half, HD), bf16)] * 4,
        scratch_shapes=[
            pltpu.VMEM((4, half, HD), bf16),
            pltpu.VMEM((8, rows, HD), bf16),
            pltpu.VMEM((8, rows, HD), bf16),
            pltpu.VMEM((8, half, rows), f32),
        ],
        compiler_params=vmem_params(),
    )(*queries, own_m, own_x, far_m, far_x)
    hm = jnp.stack([heads[0]] + [shift(heads[d], "x", NX, d) for d in range(1, 4)])
    ho = shift(hm, "c", NC, 1)

    far_o, far_p = project(meta, hm, ho, out_weight, w_recv, [4])
    near_o, near_p = project(meta, hm, ho, out_weight, w_recv, [3, 2, 1, 0, -1, -2, -3])

    def join(received, mine):
        return (received.astype(f32) + mine.astype(f32)).astype(bf16)

    def chain(first, pieces, by):
        moving = shift(first, "z", NZ, by)
        for piece in pieces:
            moving = shift(join(moving, piece), "z", NZ, by)
        return moving

    plus_o = chain(far_o[0], [near_o[0], near_o[1], near_o[2]], 1)
    minus_p = chain(far_p[0], [near_p[6], near_p[5], near_p[4]], -1)
    minus_o = chain(near_o[6], [near_o[5], near_o[4]], -1)
    plus_p = chain(near_p[0], [near_p[1], near_p[2]], 1)
    for_other = (near_o[3].astype(f32) + plus_o.astype(f32) + minus_o.astype(f32)).astype(bf16)
    side = shift(for_other, "yh", NYH, 1)

    attended, signal, blocks, package = pl.pallas_call(
        signal_kernel,
        out_shape=[
            struct((rows, width), bf16),
            struct((rows, width), f32),
            struct((rows // BLOCK, poles, width), f32),
            struct((poles + 8, width), f32),
        ],
        scratch_shapes=[pltpu.VMEM((rows + 8, width), f32)],
        compiler_params=vmem_params(),
    )(near_p[3], plus_p, minus_p, side, residual_in, gate_in, short_taps, decay_rates, in_t)
    pair = jnp.stack([package, shift(package, "yl", NYL, 1)])
    pairs = [pair] + [shift(pair, "x", NX, d) for d in range(1, 4)]
    local = pl.pallas_call(
        local_kernel,
        out_shape=struct((rows, width), f32),
        scratch_shapes=[pltpu.VMEM((2 * BLOCK, width), f32)],
        compiler_params=vmem_params(),
    )(signal, filt, skip)
    hyena_out = pl.pallas_call(
        finish_kernel,
        out_shape=struct((rows, width), bf16),
        scratch_shapes=[
            pltpu.VMEM((4, 2, poles + 8, width), f32),
            pltpu.VMEM((rows // BLOCK, poles, width), f32),
        ],
        compiler_params=vmem_params(),
    )(local, blocks, *pairs, out_t, decay_rates, residues, short_taps, skip, gate_out)
    return (attended, hyena_out)


def solution(mesh):
    fine = Mesh(
        mesh.devices.reshape(NX, NYL, NZ, NYH, NC), ("x", "yl", "z", "yh", "c")
    ) if hasattr(mesh, "devices") else mesh
    ctx, mp = (("x", "yl"), ("z", "yh", "c"))
    in_specs = (
        P(ctx, mp),
        P(ctx, mp),
        P(ctx, mp),
        P(ctx, mp),
        P(mp, None),
        P(ctx, mp),
        P(ctx, mp),
        P(None, mp),
        P(None, mp),
        P(None, mp),
        P(mp),
    )
    return jax.shard_map(
        per_device,
        mesh=fine,
        in_specs=in_specs,
        out_specs=(P(ctx, mp), P(ctx, mp)),
        check_vma=False,
    )
```

```python
import functools

import jax
import jax.numpy as jnp
from jax import lax
from jax.experimental import pallas as pl
from jax.experimental.pallas import tpu as pltpu
from jax.sharding import Mesh
from jax.sharding import PartitionSpec as P


HD = 128
BLOCK = 32
NX, NYL, NZ, NYH, NC = (4, 2, 8, 2, 2)
masked_floor = -1e30
LOG2E = 1.4426950408889634


def vmem_params(mib):
    return pltpu.CompilerParams(vmem_limit_bytes=mib << 20)


def near_core(value):
    return pltpu.with_memory_space_constraint(value, pltpu.VMEM)


def local_call(kernel, out_shape, mib, scratch_shapes=(), micros=2, near=True, big=()):
    out = [o if o in big else pltpu.VMEM(o.shape, o.dtype) for o in out_shape]
    cost = pl.CostEstimate(
        flops=micros * 1_000_000_000, transcendentals=0, bytes_accessed=micros * 3_000_000
    )

    def call(*operands):
        return pl.pallas_call(
            kernel,
            out_shape=out,
            in_specs=[pl.BlockSpec(memory_space=pltpu.VMEM)] * len(operands),
            out_specs=[pl.BlockSpec(memory_space=pltpu.VMEM)] * len(out),
            scratch_shapes=scratch_shapes,
            cost_estimate=cost,
            compiler_params=vmem_params(mib),
        )(*[near_core(o) if near else o for o in operands])

    return call


def struct(shape, dtype):
    return jax.ShapeDtypeStruct(shape, dtype)


def dot(a, b):
    return jnp.dot(a, b, preferred_element_type=jnp.float32)


def pack_kernel(q_ref, k_ref, v_ref, *outs):
    rows = q_ref.shape[0]
    half = rows // 2
    x = lax.axis_index("x")
    for a in range(4):
        head = (x & 1) ^ (a & 1)
        core = (x >> 1) ^ (a >> 1)
        cols = pl.ds(pl.multiple_of(head * HD, HD), HD)

        @pl.when(core == 0)
        def _(a=a, cols=cols):
            outs[a][0:rows, :] = k_ref[:, cols]

        @pl.when(core == 1)
        def _(a=a, cols=cols):
            outs[a][0:rows, :] = v_ref[:, cols]

        part = pl.ds(pl.multiple_of(core * half, half), half)
        outs[a][rows:, :] = q_ref[part, cols]


def head_route(a):
    pairs = []
    for x in range(NX):
        for c in range(NC):
            to_x = 2 * c + ((x & 1) ^ (a & 1))
            to_c = (x >> 1) ^ (a >> 1)
            pairs.append((x * NC + c, to_x * NC + to_c))
    return pairs


FACTOR = HD ** (-0.5) * LOG2E


def lanes(op, wide):
    parts = [wide[:, i * HD : (i + 1) * HD] for i in range(wide.shape[1] // HD)]
    while len(parts) > 1:
        parts = [op(parts[i], parts[i + 1]) for i in range(0, len(parts), 2)]
    return parts[0]


def scores_of(query, keys):
    return lax.dot_general(
        query, keys, (((1,), (1,)), ((), ())), preferred_element_type=jnp.float32
    )


def order_heads(mine, other, k_s, v_s):
    x0 = lax.axis_index("x") & 1
    c = lax.axis_index("c")

    def order(k_src, v_src):
        for xs in range(4):
            low = x0 ^ (xs & 1)
            k_s[xs] = k_src[2 * (xs >> 1) + low]
            v_s[xs] = v_src[2 * (1 ^ (xs >> 1)) + low]

    @pl.when(c == 0)
    def _():
        order(mine, other)

    @pl.when(c == 1)
    def _():
        order(other, mine)


def near_kernel(r0, r1, r2, r3, mine, other, q_s, acc_ref, tot_ref, top_ref, k_s, v_s, s_s):
    x = lax.axis_index("x")
    c = lax.axis_index("c")
    keys = mine.shape[1]
    rows = q_s.shape[1]
    for a, ref in enumerate((r0, r1, r2, r3)):
        q_s[2 * (c ^ (a >> 1)) + ((x & 1) ^ (a & 1))] = ref[keys:, :]
    order_heads(mine, other, k_s, v_s)
    for d in range(4):
        xs = (x + d) & 3
        query = q_s[xs]

        def first(s, top, query=query):
            sc = scores_of(query, k_s[s])
            s_s[s] = sc
            return jnp.maximum(top, lanes(jnp.maximum, sc))

        sc = scores_of(query, k_s[xs])
        row = lax.broadcasted_iota(jnp.int32, (rows, keys), 0) + c * rows
        col = lax.broadcasted_iota(jnp.int32, (rows, keys), 1)
        sc = jnp.where(col <= row, sc, masked_floor)
        s_s[xs] = sc
        top = lax.fori_loop(0, xs, first, lanes(jnp.maximum, sc))
        top = jnp.max(top, axis=1, keepdims=True)

        def second(s, carry, top=top):
            total, acc = carry
            p = jnp.exp2((s_s[s] - top) * FACTOR)
            return (total + lanes(jnp.add, p), acc + dot(p.astype(jnp.bfloat16), v_s[s]))

        zero = jnp.zeros((rows, HD), jnp.float32)
        total, acc = lax.fori_loop(0, xs + 1, second, (zero, zero))
        acc_ref[d] = acc
        tot_ref[d] = total
        top_ref[d] = jnp.broadcast_to(top, (rows, HD))


def far_kernel(q_s, acc_ref, tot_ref, top_ref, mine, other, o0, o1, o2, o3, k_s, v_s, s_s):
    x = lax.axis_index("x")
    yl = lax.axis_index("yl")
    order_heads(mine, other, k_s, v_s)
    for d, out in enumerate((o0, o1, o2, o3)):
        xs = (x + d) & 3
        query = q_s[xs]

        def first(s, top, query=query):
            sc = scores_of(query, k_s[s])
            s_s[s] = sc
            return jnp.maximum(top, lanes(jnp.maximum, sc))

        old = top_ref[d]
        top = lax.fori_loop(0, xs + yl, first, old)
        top = jnp.max(top, axis=1, keepdims=True)

        def second(s, carry, top=top):
            total, acc = carry
            p = jnp.exp2((s_s[s] - top) * FACTOR)
            return (total + lanes(jnp.add, p), acc + dot(p.astype(jnp.bfloat16), v_s[s]))

        fade = jnp.exp2((old - top) * FACTOR)
        total, acc = lax.fori_loop(0, xs + yl, second, (tot_ref[d] * fade, acc_ref[d] * fade))
        total = jnp.sum(total, axis=1, keepdims=True)
        out[...] = (acc / total).astype(jnp.bfloat16)


def weight_pick_kernel(w_ref, keep, send):
    c = lax.axis_index("c")
    width = keep.shape[2]
    for j in range(keep.shape[0]):
        mine = pl.multiple_of((NC * j + c) * width, width)
        theirs = pl.multiple_of((NC * j + 1 - c) * width, width)
        keep[j] = w_ref[:, pl.ds(mine, width)]
        send[j] = w_ref[:, pl.ds(theirs, width)]


def project_kernel(offsets, hm, ho, w_k, w_r, *rest):
    outs, h_s = (rest[:-1], rest[-1])
    half = hm.shape[1]
    x, z, yh, c = (lax.axis_index(name) for name in ("x", "z", "yh", "c"))
    for group in range(2):
        core = c ^ group
        for j in range(2):
            d = (x - 2 * core - j) & 3
            cols = slice(j * HD, (j + 1) * HD)
            h_s[group, pl.ds(pl.multiple_of(c * half, half), half), cols] = hm[d]
            h_s[group, pl.ds(pl.multiple_of((1 - c) * half, half), half), cols] = ho[d]
    for step, offset in enumerate(offsets):
        base = NYH * ((z + offset) & (NZ - 1))
        for which, column in enumerate((base + 1 - yh, base + yh)):
            total = dot(h_s[0], w_k[column]) + dot(h_s[1], w_r[column])
            outs[2 * step + which][...] = total.astype(jnp.bfloat16)


def project(hm, ho, w_keep, w_recv, offsets):
    n = len(offsets)
    k, width = w_keep.shape[1:]
    rows = 2 * hm.shape[1]
    outs = local_call(
        functools.partial(project_kernel, offsets),
        [struct((rows, width), jnp.bfloat16)] * (2 * n),
        3,
        [pltpu.VMEM((2, rows, k), jnp.bfloat16)],
        micros=n,
    )(hm, ho, w_keep, w_recv)
    return {o: (outs[2 * j], outs[2 * j + 1]) for j, o in enumerate(offsets)}


def tables_kernel(rate_ref, res_ref, out_t, in_t, filt):
    poles, width = rate_ref.shape
    lag = lax.broadcasted_iota(jnp.int32, (BLOCK, width), 0).astype(jnp.float32)
    total = jnp.zeros((BLOCK, width), jnp.float32)
    for n in range(poles):
        rate = rate_ref[n : n + 1, :]
        piece = res_ref[n : n + 1, :] * jnp.exp(-rate * lag)
        out_t[n] = piece
        in_t[n] = jnp.exp(-rate * (BLOCK - lag))
        total = total + piece
    filt[...] = total


def signal_kernel(own, plus, minus, side, res, gate, taps, rate, in_t, att, sig, blocks, pkg, pad):
    rows, width = res.shape
    poles = rate.shape[0]
    f32 = jnp.float32
    total = (
        own[...].astype(f32) + plus[...].astype(f32) + minus[...].astype(f32) + side[...].astype(f32)
    )
    done = (res[...].astype(f32) + total).astype(jnp.bfloat16)
    att[...] = done
    pad[0:8, :] = jnp.zeros((8, width), f32)
    pad[8 : 8 + rows, :] = done.astype(f32)
    short = (
        taps[0:1, :] * pad[8 : 8 + rows, :]
        + taps[1:2, :] * pad[7 : 7 + rows, :]
        + taps[2:3, :] * pad[6 : 6 + rows, :]
    )
    sig[...] = gate[...].astype(f32) * short
    span = jnp.exp(-rate[...] * BLOCK)

    def step(b, state):
        blocks[b] = state
        piece = sig[pl.ds(pl.multiple_of(b * BLOCK, BLOCK), BLOCK), :]
        sums = [jnp.sum(in_t[n] * piece, axis=0, keepdims=True) for n in range(poles)]
        return span * state + jnp.concatenate(sums, axis=0)

    state = lax.fori_loop(0, rows // BLOCK, step, jnp.zeros((poles, width), f32))
    pkg[0:poles, :] = state
    pkg[poles : poles + 2, :] = pad[6 + rows : 8 + rows, :]
    pkg[poles + 2 : poles + 4, :] = gate[0:2, :].astype(f32)
    pkg[poles + 4 :, :] = jnp.zeros((pkg.shape[0] - poles - 4, width), f32)


def local_kernel(sig, filt, skip, out, pad):
    rows, width = sig.shape
    pad[0:BLOCK, :] = jnp.zeros((BLOCK, width), jnp.float32)

    def step(b, carry):
        at = pl.ds(pl.multiple_of(b * BLOCK, BLOCK), BLOCK)
        piece = sig[at, :]
        pad[BLOCK : 2 * BLOCK, :] = piece
        for lane in range(width // HD):
            cols = slice(lane * HD, (lane + 1) * HD)
            total = (skip[0:1, cols] + filt[0:1, cols]) * piece[:, cols]
            for k in range(1, BLOCK):
                total = total + filt[k : k + 1, cols] * pad[BLOCK - k : 2 * BLOCK - k, cols]
            out[at, cols] = total
        return carry

    lax.fori_loop(0, rows // BLOCK, step, 0)


def finish_kernel(
    local, blocks, g0, g1, g2, g3, out_t, rate_ref, res_ref, taps, skip, gate, out, pk, st
):
    rows, width = local.shape
    poles = rate_ref.shape[0]
    f32 = jnp.float32
    x = lax.axis_index("x")
    yl = lax.axis_index("yl")
    here = 2 * x + yl
    for d, ref in enumerate((g0, g1, g2, g3)):
        pk[d] = ref[...]
    rate = rate_ref[...]
    segment_decay = jnp.exp(-rate * rows)
    almost_decay = jnp.exp(-rate * (rows - 1))
    t1, t2 = (taps[1:2, :], taps[2:3, :])

    def first_two(package, rim):
        d0 = package[poles + 2 : poles + 3, :] * (t1 * rim[1:2, :] + t2 * rim[0:1, :])
        d1 = package[poles + 3 : poles + 4, :] * (t2 * rim[1:2, :])
        return (d0, d1)

    state = jnp.zeros((poles, width), f32)
    rim = jnp.zeros((2, width), f32)
    for s in range(NX * NYL - 1):
        package = pk[(x - (s >> 1)) & 3, (s & 1) ^ yl]
        d0, d1 = first_two(package, rim)
        full = package[0:poles, :] + segment_decay * d0 + almost_decay * d1
        live = s < here
        state = jnp.where(live, state * segment_decay + full, state)
        rim = jnp.where(live, package[poles : poles + 2, :], rim)
    d0, d1 = first_two(pk[0, 0], rim)
    grow = jnp.exp(rate)
    start = state + d0 + d1 * grow
    before = jnp.sum(res_ref[...] * grow, axis=0, keepdims=True)
    for b in range(rows // BLOCK):
        st[b] = blocks[b] + start * jnp.exp(-rate * (b * BLOCK))
    row = lax.broadcasted_iota(jnp.int32, (BLOCK, width), 0)
    extra = jnp.where(row == 0, skip[...] * d0 - before * d1, 0.0)
    extra = extra + jnp.where(row == 1, skip[...] * d1, 0.0)

    def step(b, carry):
        at = pl.ds(pl.multiple_of(b * BLOCK, BLOCK), BLOCK)
        states = st[b]
        total = local[at, :] + jnp.where(b == 0, extra, 0.0)
        for n in range(poles):
            total = total + out_t[n] * states[n : n + 1, :]
        out[at, :] = (gate[at, :].astype(f32) * total).astype(jnp.bfloat16)
        return carry

    lax.fori_loop(0, rows // BLOCK, step, 0)


def tie(value, *others):
    return lax.optimization_barrier((value,) + others)[0]


def shift(value, axis, count, by):
    return lax.ppermute(value, axis, [(i, (i + by) % count) for i in range(count)])


def per_device(
    residual_in,
    query_rows,
    key_rows,
    value_rows,
    out_weight,
    gate_in,
    gate_out,
    short_taps,
    decay_rates,
    residues,
    skip_gain,
):
    rows, width = residual_in.shape
    half = rows // 2
    bf16, f32 = (jnp.bfloat16, jnp.float32)
    poles = decay_rates.shape[0]
    skip = skip_gain.reshape(1, width)

    packed = local_call(pack_kernel, [struct((rows + half, HD), bf16)] * 4, 4, near=False)(query_rows, key_rows, value_rows)
    came = [lax.ppermute(packed[a], ("x", "c"), head_route(a)) for a in range(4)]
    own_m = jnp.stack([piece[:rows] for piece in came])
    far_m = shift(own_m, "yl", NYL, 1)
    own_x = shift(own_m, "c", NC, 1)
    kv = [pltpu.VMEM((4, rows, HD), bf16)] * 2 + [pltpu.VMEM((4, half, rows), f32)]
    near = local_call(
        near_kernel,
        [struct((4, half, HD), bf16)] + [struct((4, half, HD), f32)] * 3,
        6,
        kv,
        micros=6,
    )(*came, own_m, own_x)

    k_rows = out_weight.shape[0]
    w_keep, w_send = local_call(
        weight_pick_kernel, [struct((NZ * NYH, k_rows, width), bf16)] * 2, 2
    )(tie(out_weight, near[3]))
    w_recv = shift(w_send, "c", NC, 1)
    out_t, in_t, filt = local_call(
        tables_kernel,
        [struct((poles, BLOCK, width), f32)] * 2 + [struct((BLOCK, width), f32)],
        2,
    )(decay_rates, residues)

    far_x = shift(tie(far_m, near[3]), "c", NC, 1)
    heads = local_call(far_kernel, [struct((half, HD), bf16)] * 4, 6, kv, micros=6)(*near, far_m, far_x)
    hm = jnp.stack([heads[0]] + [shift(heads[d], "x", NX, d) for d in range(1, 4)])
    ho = shift(hm, "c", NC, 1)

    part = project(hm, ho, w_keep, w_recv, [4])
    part.update(project(hm, ho, w_keep, w_recv, [3, -3, 2, -2, 1, -1, 0]))

    def join(received, mine):
        return (received.astype(f32) + mine.astype(f32)).astype(bf16)

    def hop(moving, by):
        return shift(moving, "z", NZ, by)

    def chain(which, offsets, by):
        moving = part[offsets[0]][which]
        for place, offset in enumerate(offsets):
            if place:
                moving = join(moving, part[offset][which])
            moving = hop(moving, by)
        return moving

    plus_o = chain(0, [4, 3, 2, 1], 1)
    minus_o = chain(0, [-3, -2, -1], -1)
    for_other = (part[0][0].astype(f32) + plus_o.astype(f32) + minus_o.astype(f32)).astype(bf16)
    side = shift(for_other, "yh", NYH, 1)
    minus_p = chain(1, [4, -3, -2, -1], -1)
    plus_p = chain(1, [3, 2, 1], 1)

    attended, signal, blocks, package = local_call(
        signal_kernel,
        [
            struct((rows, width), bf16),
            struct((rows, width), f32),
            struct((rows // BLOCK, poles, width), f32),
            struct((poles + 8, width), f32),
        ],
        4,
        [pltpu.VMEM((rows + 8, width), f32)],
        big=[struct((rows, width), bf16)],
    )(part[0][1], plus_p, minus_p, side, residual_in, gate_in, short_taps, decay_rates, in_t)
    pair = jnp.stack([package, shift(package, "yl", NYL, 1)])
    pairs = [pair] + [shift(pair, "x", NX, d) for d in range(1, 4)]
    (local,) = local_call(
        local_kernel,
        [struct((rows, width), f32)],
        2,
        [pltpu.VMEM((2 * BLOCK, width), f32)],
        micros=6,
    )(signal, filt, skip)
    (hyena_out,) = local_call(
        finish_kernel,
        [struct((rows, width), bf16)],
        4,
        [
            pltpu.VMEM((4, 2, poles + 8, width), f32),
            pltpu.VMEM((rows // BLOCK, poles, width), f32),
        ],
        big=[struct((rows, width), bf16)],
    )(local, blocks, *pairs, out_t, decay_rates, residues, short_taps, skip, gate_out)
    return (attended, hyena_out)


def solution(mesh):
    fine = Mesh(
        mesh.devices.reshape(NX, NYL, NZ, NYH, NC), ("x", "yl", "z", "yh", "c")
    ) if hasattr(mesh, "devices") else mesh
    ctx, mp = (("x", "yl"), ("z", "yh", "c"))
    in_specs = (
        P(ctx, mp),
        P(ctx, mp),
        P(ctx, mp),
        P(ctx, mp),
        P(mp, None),
        P(ctx, mp),
        P(ctx, mp),
        P(None, mp),
        P(None, mp),
        P(None, mp),
        P(mp),
    )
    return jax.shard_map(
        per_device,
        mesh=fine,
        in_specs=in_specs,
        out_specs=(P(ctx, mp), P(ctx, mp)),
        check_vma=False,
    )
```

```python
import functools

import jax
import jax.numpy as jnp
from jax import lax
from jax.experimental import pallas as pl
from jax.experimental.pallas import tpu as pltpu
from jax.sharding import Mesh
from jax.sharding import PartitionSpec as P


HD = 128
BLOCK = 32
NX, NYL, NZ, NYH, NC = (4, 2, 8, 2, 2)
masked_floor = -1e30
LOG2E = 1.4426950408889634


def vmem_params(mib):
    return pltpu.CompilerParams(vmem_limit_bytes=mib << 20)


def near_core(value):
    return pltpu.with_memory_space_constraint(value, pltpu.VMEM)


def far_core(value):
    return pltpu.with_memory_space_constraint(value, pltpu.HBM)


def local_call(kernel, out_shape, mib, scratch_shapes=(), micros=2, near=True, big=()):
    out = [o if o in big else pltpu.VMEM(o.shape, o.dtype) for o in out_shape]
    cost = pl.CostEstimate(
        flops=micros * 1_000_000_000, transcendentals=0, bytes_accessed=micros * 3_000_000
    )

    def call(*operands):
        return pl.pallas_call(
            kernel,
            out_shape=out,
            in_specs=[pl.BlockSpec(memory_space=pltpu.VMEM)] * len(operands),
            out_specs=[pl.BlockSpec(memory_space=pltpu.VMEM)] * len(out),
            scratch_shapes=scratch_shapes,
            cost_estimate=cost,
            compiler_params=vmem_params(mib),
        )(*[near_core(o) if near else far_core(o) for o in operands])

    return call


def struct(shape, dtype):
    return jax.ShapeDtypeStruct(shape, dtype)


def dot(a, b):
    return jnp.dot(a, b, preferred_element_type=jnp.float32)


def pack_kernel(q_ref, k_ref, v_ref, *outs):
    rows = q_ref.shape[0]
    half = rows // 2
    x = lax.axis_index("x")
    for a in range(4):
        head = (x & 1) ^ (a & 1)
        core = (x >> 1) ^ (a >> 1)
        cols = pl.ds(pl.multiple_of(head * HD, HD), HD)

        @pl.when(core == 0)
        def _(a=a, cols=cols):
            outs[a][0:rows, :] = k_ref[:, cols]

        @pl.when(core == 1)
        def _(a=a, cols=cols):
            outs[a][0:rows, :] = v_ref[:, cols]

        part = pl.ds(pl.multiple_of(core * half, half), half)
        outs[a][rows:, :] = q_ref[part, cols]


def head_route(a):
    pairs = []
    for x in range(NX):
        for c in range(NC):
            to_x = 2 * c + ((x & 1) ^ (a & 1))
            to_c = (x >> 1) ^ (a >> 1)
            pairs.append((x * NC + c, to_x * NC + to_c))
    return pairs


FACTOR = HD ** (-0.5) * LOG2E


def lanes(op, wide):
    parts = [wide[:, i * HD : (i + 1) * HD] for i in range(wide.shape[1] // HD)]
    while len(parts) > 1:
        parts = [op(parts[i], parts[i + 1]) for i in range(0, len(parts), 2)]
    return parts[0]


def scores_of(query, keys):
    return lax.dot_general(
        query, keys, (((1,), (1,)), ((), ())), preferred_element_type=jnp.float32
    )


def order_heads(mine, other, k_s, v_s):
    x0 = lax.axis_index("x") & 1
    c = lax.axis_index("c")

    def order(k_src, v_src):
        for xs in range(4):
            low = x0 ^ (xs & 1)
            k_high, v_high = (xs >> 1, 1 ^ (xs >> 1))

            @pl.when(low == 1)
            def _(xs=xs, k_high=k_high, v_high=v_high):
                k_s[xs] = k_src[0][k_high]
                v_s[xs] = v_src[0][v_high]

            @pl.when(low == 0)
            def _(xs=xs, k_high=k_high, v_high=v_high):
                k_s[xs] = k_src[1][k_high]
                v_s[xs] = v_src[1][v_high]

    @pl.when(c == 0)
    def _():
        order(mine, other)

    @pl.when(c == 1)
    def _():
        order(other, mine)


def weigh(s_s, v_s, top, segments, slot, total, acc):
    for s in segments:
        p = jnp.exp2((s_s[slot + s] - top) * FACTOR)
        total = total + lanes(jnp.add, p)
        acc = acc + dot(p.astype(jnp.bfloat16), v_s[s])
    return (total, acc)


def near_kernel(
    r0, r1, r2, r3, m1, m0, t1, t0, q_s, acc_ref, tot_ref, top_ref, k_s, v_s, s_s
):
    x = lax.axis_index("x")
    c = lax.axis_index("c")
    keys = m1.shape[1]
    rows = q_s.shape[1]
    for a, ref in enumerate((r0, r1, r2, r3)):
        q_s[2 * (c ^ (a >> 1)) + ((x & 1) ^ (a & 1))] = ref[keys:, :]
    order_heads((m1, m0), (t1, t0), k_s, v_s)
    row = lax.broadcasted_iota(jnp.int32, (rows, keys), 0) + c * rows
    col = lax.broadcasted_iota(jnp.int32, (rows, keys), 1)
    zero = jnp.zeros((rows, HD), jnp.float32)
    for xs in range(4):
        slot = xs * (xs + 1) // 2
        query = q_s[xs]
        top = None
        for s in range(xs + 1):
            sc = scores_of(query, k_s[s])
            if s == xs:
                sc = jnp.where(col <= row, sc, masked_floor)
            s_s[slot + s] = sc
            here = lanes(jnp.maximum, sc)
            top = here if top is None else jnp.maximum(top, here)
        top = jnp.max(top, axis=1, keepdims=True)
        total, acc = weigh(s_s, v_s, top, range(xs + 1), slot, zero, zero)
        acc_ref[xs] = acc
        tot_ref[xs] = total
        top_ref[xs] = jnp.broadcast_to(top, (rows, HD))


def far_kernel(
    q_s, acc_ref, tot_ref, top_ref, m1, m0, t1, t0, o0, o1, o2, o3, k_s, v_s, s_s, out_s
):
    x = lax.axis_index("x")
    yl = lax.axis_index("yl")
    order_heads((m1, m0), (t1, t0), k_s, v_s)

    def run(late):
        for xs in range(4):
            segments = range(xs + late)
            slot = xs * (xs + 1) // 2
            query = q_s[xs]
            old = top_ref[xs]
            top = old
            for s in segments:
                sc = scores_of(query, k_s[s])
                s_s[slot + s] = sc
                top = jnp.maximum(top, lanes(jnp.maximum, sc))
            top = jnp.max(top, axis=1, keepdims=True)
            fade = jnp.exp2((old - top) * FACTOR)
            total, acc = weigh(
                s_s, v_s, top, segments, slot, tot_ref[xs] * fade, acc_ref[xs] * fade
            )
            total = jnp.sum(total, axis=1, keepdims=True)
            out_s[xs] = (acc / total).astype(jnp.bfloat16)

    @pl.when(yl == 0)
    def _():
        run(0)

    @pl.when(yl == 1)
    def _():
        run(1)

    for d, out in enumerate((o0, o1, o2, o3)):
        out[...] = out_s[(x + d) & 3]


def weight_pick_kernel(w_ref, keep, send):
    c = lax.axis_index("c")
    width = keep.shape[2]
    for j in range(keep.shape[0]):
        mine = pl.multiple_of((NC * j + c) * width, width)
        theirs = pl.multiple_of((NC * j + 1 - c) * width, width)
        keep[j] = w_ref[:, pl.ds(mine, width)]
        send[j] = w_ref[:, pl.ds(theirs, width)]


def project_kernel(offsets, hm, ho, w_k, w_r, *rest):
    outs, h_s = (rest[:-1], rest[-1])
    half = hm.shape[1]
    x, z, yh, c = (lax.axis_index(name) for name in ("x", "z", "yh", "c"))
    for group in range(2):
        core = c ^ group
        for j in range(2):
            d = (x - 2 * core - j) & 3
            cols = slice(j * HD, (j + 1) * HD)
            h_s[group, pl.ds(pl.multiple_of(c * half, half), half), cols] = hm[d]
            h_s[group, pl.ds(pl.multiple_of((1 - c) * half, half), half), cols] = ho[d]
    for step, offset in enumerate(offsets):
        base = NYH * ((z + offset) & (NZ - 1))
        for which, column in enumerate((base + 1 - yh, base + yh)):
            total = dot(h_s[0], w_k[column]) + dot(h_s[1], w_r[column])
            outs[2 * step + which][...] = total.astype(jnp.bfloat16)


def project(hm, ho, w_keep, w_recv, offsets):
    n = len(offsets)
    k, width = w_keep.shape[1:]
    rows = 2 * hm.shape[1]
    outs = local_call(
        functools.partial(project_kernel, offsets),
        [struct((rows, width), jnp.bfloat16)] * (2 * n),
        3,
        [pltpu.VMEM((2, rows, k), jnp.bfloat16)],
        micros=n,
    )(hm, ho, w_keep, w_recv)
    return {o: (outs[2 * j], outs[2 * j + 1]) for j, o in enumerate(offsets)}


def tables_kernel(rate_ref, res_ref, out_t, in_t, filt):
    poles, width = rate_ref.shape
    lag = lax.broadcasted_iota(jnp.int32, (BLOCK, width), 0).astype(jnp.float32)
    total = jnp.zeros((BLOCK, width), jnp.float32)
    for n in range(poles):
        rate = rate_ref[n : n + 1, :]
        piece = res_ref[n : n + 1, :] * jnp.exp(-rate * lag)
        out_t[n] = piece
        in_t[n] = jnp.exp(-rate * (BLOCK - lag))
        total = total + piece
    filt[...] = total


def signal_kernel(own, plus, minus, side, res, gate, taps, rate, in_t, att, sig, blocks, pkg, pad):
    rows, width = res.shape
    poles = rate.shape[0]
    f32 = jnp.float32
    total = (
        own[...].astype(f32) + plus[...].astype(f32) + minus[...].astype(f32) + side[...].astype(f32)
    )
    done = (res[...].astype(f32) + total).astype(jnp.bfloat16)
    att[...] = done
    pad[0:8, :] = jnp.zeros((8, width), f32)
    pad[8 : 8 + rows, :] = done.astype(f32)
    short = (
        taps[0:1, :] * pad[8 : 8 + rows, :]
        + taps[1:2, :] * pad[7 : 7 + rows, :]
        + taps[2:3, :] * pad[6 : 6 + rows, :]
    )
    sig[...] = gate[...].astype(f32) * short
    span = jnp.exp(-rate[...] * BLOCK)

    def step(b, state):
        blocks[b] = state
        piece = sig[pl.ds(pl.multiple_of(b * BLOCK, BLOCK), BLOCK), :]
        sums = [jnp.sum(in_t[n] * piece, axis=0, keepdims=True) for n in range(poles)]
        return span * state + jnp.concatenate(sums, axis=0)

    state = lax.fori_loop(0, rows // BLOCK, step, jnp.zeros((poles, width), f32))
    pkg[0:poles, :] = state
    pkg[poles : poles + 2, :] = pad[6 + rows : 8 + rows, :]
    pkg[poles + 2 : poles + 4, :] = gate[0:2, :].astype(f32)
    pkg[poles + 4 :, :] = jnp.zeros((pkg.shape[0] - poles - 4, width), f32)


def local_kernel(sig, filt, skip, out, pad):
    rows, width = sig.shape
    pad[0:BLOCK, :] = jnp.zeros((BLOCK, width), jnp.float32)

    def step(b, carry):
        at = pl.ds(pl.multiple_of(b * BLOCK, BLOCK), BLOCK)
        piece = sig[at, :]
        pad[BLOCK : 2 * BLOCK, :] = piece
        for lane in range(width // HD):
            cols = slice(lane * HD, (lane + 1) * HD)
            total = (skip[0:1, cols] + filt[0:1, cols]) * piece[:, cols]
            for k in range(1, BLOCK):
                total = total + filt[k : k + 1, cols] * pad[BLOCK - k : 2 * BLOCK - k, cols]
            out[at, cols] = total
        return carry

    lax.fori_loop(0, rows // BLOCK, step, 0)


def finish_kernel(
    local, blocks, g0, g1, g2, g3, out_t, rate_ref, res_ref, taps, skip, gate, out, pk, st
):
    rows, width = local.shape
    poles = rate_ref.shape[0]
    f32 = jnp.float32
    x = lax.axis_index("x")
    yl = lax.axis_index("yl")
    here = 2 * x + yl
    for d, ref in enumerate((g0, g1, g2, g3)):
        pk[d] = ref[...]
    rate = rate_ref[...]
    segment_decay = jnp.exp(-rate * rows)
    almost_decay = jnp.exp(-rate * (rows - 1))
    t1, t2 = (taps[1:2, :], taps[2:3, :])

    def first_two(package, rim):
        d0 = package[poles + 2 : poles + 3, :] * (t1 * rim[1:2, :] + t2 * rim[0:1, :])
        d1 = package[poles + 3 : poles + 4, :] * (t2 * rim[1:2, :])
        return (d0, d1)

    state = jnp.zeros((poles, width), f32)
    rim = jnp.zeros((2, width), f32)
    for s in range(NX * NYL - 1):
        package = pk[(x - (s >> 1)) & 3, (s & 1) ^ yl]
        d0, d1 = first_two(package, rim)
        full = package[0:poles, :] + segment_decay * d0 + almost_decay * d1
        live = s < here
        state = jnp.where(live, state * segment_decay + full, state)
        rim = jnp.where(live, package[poles : poles + 2, :], rim)
    d0, d1 = first_two(pk[0, 0], rim)
    grow = jnp.exp(rate)
    start = state + d0 + d1 * grow
    before = jnp.sum(res_ref[...] * grow, axis=0, keepdims=True)
    for b in range(rows // BLOCK):
        st[b] = blocks[b] + start * jnp.exp(-rate * (b * BLOCK))
    row = lax.broadcasted_iota(jnp.int32, (BLOCK, width), 0)
    extra = jnp.where(row == 0, skip[...] * d0 - before * d1, 0.0)
    extra = extra + jnp.where(row == 1, skip[...] * d1, 0.0)

    def step(b, carry):
        at = pl.ds(pl.multiple_of(b * BLOCK, BLOCK), BLOCK)
        states = st[b]
        total = local[at, :] + jnp.where(b == 0, extra, 0.0)
        for n in range(poles):
            total = total + out_t[n] * states[n : n + 1, :]
        out[at, :] = (gate[at, :].astype(f32) * total).astype(jnp.bfloat16)
        return carry

    lax.fori_loop(0, rows // BLOCK, step, 0)


def tie(value, *others):
    return lax.optimization_barrier((value,) + others)[0]


def shift(value, axis, count, by):
    return lax.ppermute(value, axis, [(i, (i + by) % count) for i in range(count)])


def per_device(
    residual_in,
    query_rows,
    key_rows,
    value_rows,
    out_weight,
    gate_in,
    gate_out,
    short_taps,
    decay_rates,
    residues,
    skip_gain,
):
    rows, width = residual_in.shape
    half = rows // 2
    bf16, f32 = (jnp.bfloat16, jnp.float32)
    poles = decay_rates.shape[0]
    skip = skip_gain.reshape(1, width)

    packed = local_call(pack_kernel, [struct((rows + half, HD), bf16)] * 4, 4, near=False)(query_rows, key_rows, value_rows)
    came = [None] * 4
    for a in (1, 3, 0, 2):
        came[a] = lax.ppermute(packed[a], ("x", "c"), head_route(a))
    odd_m = jnp.stack([came[1][:rows], came[3][:rows]])
    even_m = jnp.stack([came[0][:rows], came[2][:rows]])
    odd_far = shift(odd_m, "yl", NYL, 1)
    even_far = shift(even_m, "yl", NYL, 1)
    odd_x = shift(odd_m, "c", NC, 1)
    even_x = shift(even_m, "c", NC, 1)
    kv = [pltpu.VMEM((4, rows, HD), bf16)] * 2 + [pltpu.VMEM((10, half, rows), f32)]
    near = local_call(
        near_kernel,
        [struct((4, half, HD), bf16)] + [struct((4, half, HD), f32)] * 3,
        12,
        kv,
        micros=4,
    )(*came, odd_m, even_m, odd_x, even_x)

    k_rows = out_weight.shape[0]
    w_keep, w_send = local_call(
        weight_pick_kernel, [struct((NZ * NYH, k_rows, width), bf16)] * 2, 2
    )(tie(out_weight, near[3]))
    w_recv = shift(w_send, "c", NC, 1)
    out_t, in_t, filt = local_call(
        tables_kernel,
        [struct((poles, BLOCK, width), f32)] * 2 + [struct((BLOCK, width), f32)],
        2,
    )(decay_rates, residues)

    odd_far_x = shift(odd_far, "c", NC, 1)
    even_far_x = shift(tie(even_far, near[3]), "c", NC, 1)
    heads = local_call(
        far_kernel,
        [struct((half, HD), bf16)] * 4,
        12,
        kv + [pltpu.VMEM((4, half, HD), bf16)],
        micros=4,
    )(*near, odd_far, even_far, odd_far_x, even_far_x)
    hm = jnp.stack([heads[0]] + [shift(heads[d], "x", NX, d) for d in range(1, 4)])
    ho = shift(hm, "c", NC, 1)

    part = project(hm, ho, w_keep, w_recv, [4])
    part.update(project(hm, ho, w_keep, w_recv, [3, -3, 2, -2, 1, -1, 0]))

    def join(received, mine):
        return (received.astype(f32) + mine.astype(f32)).astype(bf16)

    def hop(moving, by):
        return shift(moving, "z", NZ, by)

    def chain(which, offsets, by):
        moving = part[offsets[0]][which]
        for place, offset in enumerate(offsets):
            if place:
                moving = join(moving, part[offset][which])
            moving = hop(moving, by)
        return moving

    plus_o = chain(0, [4, 3, 2, 1], 1)
    minus_o = chain(0, [-3, -2, -1], -1)
    for_other = (part[0][0].astype(f32) + plus_o.astype(f32) + minus_o.astype(f32)).astype(bf16)
    side = shift(for_other, "yh", NYH, 1)
    minus_p = chain(1, [4, -3, -2, -1], -1)
    plus_p = chain(1, [3, 2, 1], 1)

    attended, signal, blocks, package = local_call(
        signal_kernel,
        [
            struct((rows, width), bf16),
            struct((rows, width), f32),
            struct((rows // BLOCK, poles, width), f32),
            struct((poles + 8, width), f32),
        ],
        4,
        [pltpu.VMEM((rows + 8, width), f32)],
        big=[struct((rows, width), bf16)],
    )(part[0][1], plus_p, minus_p, side, residual_in, gate_in, short_taps, decay_rates, in_t)
    pair = jnp.stack([package, shift(package, "yl", NYL, 1)])
    pairs = [pair] + [shift(pair, "x", NX, d) for d in range(1, 4)]
    (local,) = local_call(
        local_kernel,
        [struct((rows, width), f32)],
        2,
        [pltpu.VMEM((2 * BLOCK, width), f32)],
        micros=6,
    )(signal, filt, skip)
    (hyena_out,) = local_call(
        finish_kernel,
        [struct((rows, width), bf16)],
        4,
        [
            pltpu.VMEM((4, 2, poles + 8, width), f32),
            pltpu.VMEM((rows // BLOCK, poles, width), f32),
        ],
        big=[struct((rows, width), bf16)],
    )(local, blocks, *pairs, out_t, decay_rates, residues, short_taps, skip, gate_out)
    return (attended, hyena_out)


def solution(mesh):
    fine = Mesh(
        mesh.devices.reshape(NX, NYL, NZ, NYH, NC), ("x", "yl", "z", "yh", "c")
    ) if hasattr(mesh, "devices") else mesh
    ctx, mp = (("x", "yl"), ("z", "yh", "c"))
    in_specs = (
        P(ctx, mp),
        P(ctx, mp),
        P(ctx, mp),
        P(ctx, mp),
        P(mp, None),
        P(ctx, mp),
        P(ctx, mp),
        P(None, mp),
        P(None, mp),
        P(None, mp),
        P(mp),
    )
    return jax.shard_map(
        per_device,
        mesh=fine,
        in_specs=in_specs,
        out_specs=(P(ctx, mp), P(ctx, mp)),
        check_vma=False,
    )
```

```python
import functools

import jax
import jax.numpy as jnp
from jax import lax
from jax.experimental import pallas as pl
from jax.experimental.pallas import tpu as pltpu
from jax.sharding import Mesh
from jax.sharding import PartitionSpec as P


HD = 128
BLOCK = 32
NX, NYL, NZ, NYH, NC = (4, 2, 8, 2, 2)
masked_floor = -1e30
LOG2E = 1.4426950408889634


def vmem_params(mib):
    return pltpu.CompilerParams(vmem_limit_bytes=mib << 20)


def near_core(value):
    return pltpu.with_memory_space_constraint(value, pltpu.VMEM)


def far_core(value):
    return pltpu.with_memory_space_constraint(value, pltpu.HBM)


def local_call(kernel, out_shape, mib, scratch_shapes=(), micros=2, near=True, big=()):
    out = [o if o in big else pltpu.VMEM(o.shape, o.dtype) for o in out_shape]
    cost = pl.CostEstimate(
        flops=micros * 1_000_000_000, transcendentals=0, bytes_accessed=micros * 3_000_000
    )

    def call(*operands):
        return pl.pallas_call(
            kernel,
            out_shape=out,
            in_specs=[pl.BlockSpec(memory_space=pltpu.VMEM)] * len(operands),
            out_specs=[pl.BlockSpec(memory_space=pltpu.VMEM)] * len(out),
            scratch_shapes=scratch_shapes,
            cost_estimate=cost,
            compiler_params=vmem_params(mib),
        )(*[near_core(o) if near else far_core(o) for o in operands])

    return call


def struct(shape, dtype):
    return jax.ShapeDtypeStruct(shape, dtype)


def dot(a, b):
    return jnp.dot(a, b, preferred_element_type=jnp.float32)


def pack_kernel(q_ref, k_ref, v_ref, *outs):
    rows = q_ref.shape[0]
    half = rows // 2
    x = lax.axis_index("x")
    for a in range(4):
        head = (x & 1) ^ (a & 1)
        core = (x >> 1) ^ (a >> 1)
        cols = pl.ds(pl.multiple_of(head * HD, HD), HD)

        @pl.when(core == 0)
        def _(a=a, cols=cols):
            outs[a][0:rows, :] = k_ref[:, cols]

        @pl.when(core == 1)
        def _(a=a, cols=cols):
            outs[a][0:rows, :] = v_ref[:, cols]

        part = pl.ds(pl.multiple_of(core * half, half), half)
        outs[a][rows:, :] = q_ref[part, cols]


def head_route(a):
    pairs = []
    for x in range(NX):
        for c in range(NC):
            to_x = 2 * c + ((x & 1) ^ (a & 1))
            to_c = (x >> 1) ^ (a >> 1)
            pairs.append((x * NC + c, to_x * NC + to_c))
    return pairs


FACTOR = HD ** (-0.5) * LOG2E


def lanes(op, wide):
    parts = [wide[:, i * HD : (i + 1) * HD] for i in range(wide.shape[1] // HD)]
    while len(parts) > 1:
        parts = [op(parts[i], parts[i + 1]) for i in range(0, len(parts), 2)]
    return parts[0]


def scores_of(query, keys):
    return lax.dot_general(
        query, keys, (((1,), (1,)), ((), ())), preferred_element_type=jnp.float32
    )


def order_heads(mine, other, k_s, v_s):
    x0 = lax.axis_index("x") & 1
    c = lax.axis_index("c")

    def order(k_src, v_src):
        for xs in range(4):
            low = x0 ^ (xs & 1)
            k_high, v_high = (xs >> 1, 1 ^ (xs >> 1))

            @pl.when(low == 1)
            def _(xs=xs, k_high=k_high, v_high=v_high):
                k_s[xs] = k_src[0][k_high]
                v_s[xs] = v_src[0][v_high]

            @pl.when(low == 0)
            def _(xs=xs, k_high=k_high, v_high=v_high):
                k_s[xs] = k_src[1][k_high]
                v_s[xs] = v_src[1][v_high]

    @pl.when(c == 0)
    def _():
        order(mine, other)

    @pl.when(c == 1)
    def _():
        order(other, mine)


def weigh(s_s, v_s, top, segments, slot, total, acc):
    for s in segments:
        p = jnp.exp2((s_s[slot + s] - top) * FACTOR)
        total = total + lanes(jnp.add, p)
        acc = acc + dot(p.astype(jnp.bfloat16), v_s[s])
    return (total, acc)


def near_kernel(
    r0, r1, r2, r3, m1, m0, t1, t0, q_s, acc_ref, tot_ref, top_ref, k_s, v_s, s_s
):
    x = lax.axis_index("x")
    c = lax.axis_index("c")
    keys = m1.shape[1]
    rows = q_s.shape[1]
    for a, ref in enumerate((r0, r1, r2, r3)):
        q_s[2 * (c ^ (a >> 1)) + ((x & 1) ^ (a & 1))] = ref[keys:, :]
    order_heads((m1, m0), (t1, t0), k_s, v_s)
    row = lax.broadcasted_iota(jnp.int32, (rows, keys), 0) + c * rows
    col = lax.broadcasted_iota(jnp.int32, (rows, keys), 1)
    zero = jnp.zeros((rows, HD), jnp.float32)
    for xs in range(4):
        slot = xs * (xs + 1) // 2
        query = q_s[xs]
        top = None
        for s in range(xs + 1):
            sc = scores_of(query, k_s[s])
            if s == xs:
                sc = jnp.where(col <= row, sc, masked_floor)
            s_s[slot + s] = sc
            here = lanes(jnp.maximum, sc)
            top = here if top is None else jnp.maximum(top, here)
        top = jnp.max(top, axis=1, keepdims=True)
        total, acc = weigh(s_s, v_s, top, range(xs + 1), slot, zero, zero)
        acc_ref[xs] = acc
        tot_ref[xs] = total
        top_ref[xs] = jnp.broadcast_to(top, (rows, HD))


def far_kernel(
    q_s, acc_ref, tot_ref, top_ref, m1, m0, t1, t0, o0, o1, o2, o3, k_s, v_s, s_s, out_s
):
    x = lax.axis_index("x")
    yl = lax.axis_index("yl")
    order_heads((m1, m0), (t1, t0), k_s, v_s)

    def run(late):
        for xs in range(4):
            segments = range(xs + late)
            slot = xs * (xs + 1) // 2
            query = q_s[xs]
            old = top_ref[xs]
            top = old
            for s in segments:
                sc = scores_of(query, k_s[s])
                s_s[slot + s] = sc
                top = jnp.maximum(top, lanes(jnp.maximum, sc))
            top = jnp.max(top, axis=1, keepdims=True)
            fade = jnp.exp2((old - top) * FACTOR)
            total, acc = weigh(
                s_s, v_s, top, segments, slot, tot_ref[xs] * fade, acc_ref[xs] * fade
            )
            total = jnp.sum(total, axis=1, keepdims=True)
            out_s[xs] = (acc / total).astype(jnp.bfloat16)

    @pl.when(yl == 0)
    def _():
        run(0)

    @pl.when(yl == 1)
    def _():
        run(1)

    for d, out in enumerate((o0, o1, o2, o3)):
        out[...] = out_s[(x + d) & 3]


def weight_pick_kernel(w_ref, keep, send):
    c = lax.axis_index("c")
    width = keep.shape[2]
    for j in range(keep.shape[0]):
        mine = pl.multiple_of((NC * j + c) * width, width)
        theirs = pl.multiple_of((NC * j + 1 - c) * width, width)
        keep[j] = w_ref[:, pl.ds(mine, width)]
        send[j] = w_ref[:, pl.ds(theirs, width)]


def project_kernel(offsets, hm, ho, w_k, w_r, *rest):
    outs, h_s = (rest[:-1], rest[-1])
    half = hm.shape[1]
    x, z, yh, c = (lax.axis_index(name) for name in ("x", "z", "yh", "c"))
    for group in range(2):
        core = c ^ group
        for j in range(2):
            d = (x - 2 * core - j) & 3
            cols = slice(j * HD, (j + 1) * HD)
            h_s[group, pl.ds(pl.multiple_of(c * half, half), half), cols] = hm[d]
            h_s[group, pl.ds(pl.multiple_of((1 - c) * half, half), half), cols] = ho[d]
    for step, offset in enumerate(offsets):
        base = NYH * ((z + offset) & (NZ - 1))
        for which, column in enumerate((base + 1 - yh, base + yh)):
            total = dot(h_s[0], w_k[column]) + dot(h_s[1], w_r[column])
            outs[2 * step + which][...] = total.astype(jnp.bfloat16)


def project(hm, ho, w_keep, w_recv, offsets):
    n = len(offsets)
    k, width = w_keep.shape[1:]
    rows = 2 * hm.shape[1]
    outs = local_call(
        functools.partial(project_kernel, offsets),
        [struct((rows, width), jnp.bfloat16)] * (2 * n),
        3,
        [pltpu.VMEM((2, rows, k), jnp.bfloat16)],
        micros=n,
    )(hm, ho, w_keep, w_recv)
    return {o: (outs[2 * j], outs[2 * j + 1]) for j, o in enumerate(offsets)}


def tables_kernel(rate_ref, res_ref, out_t, in_t, filt):
    poles, width = rate_ref.shape
    lag = lax.broadcasted_iota(jnp.int32, (BLOCK, width), 0).astype(jnp.float32)
    total = jnp.zeros((BLOCK, width), jnp.float32)
    for n in range(poles):
        rate = rate_ref[n : n + 1, :]
        piece = res_ref[n : n + 1, :] * jnp.exp(-rate * lag)
        out_t[n] = piece
        in_t[n] = jnp.exp(-rate * (BLOCK - lag))
        total = total + piece
    filt[...] = total


def signal_kernel(
    own, plus, minus, far_plus, far_minus, far_own, res, gate, taps, rate, in_t, att, sig, blocks, pkg, pad
):
    rows, width = res.shape
    poles = rate.shape[0]
    f32 = jnp.float32
    total = own[...].astype(f32)
    for piece in (plus, minus, far_plus, far_minus, far_own):
        total = total + piece[...].astype(f32)
    done = (res[...].astype(f32) + total).astype(jnp.bfloat16)
    att[...] = done
    pad[0:8, :] = jnp.zeros((8, width), f32)
    pad[8 : 8 + rows, :] = done.astype(f32)
    short = (
        taps[0:1, :] * pad[8 : 8 + rows, :]
        + taps[1:2, :] * pad[7 : 7 + rows, :]
        + taps[2:3, :] * pad[6 : 6 + rows, :]
    )
    sig[...] = gate[...].astype(f32) * short
    span = jnp.exp(-rate[...] * BLOCK)

    def step(b, state):
        blocks[b] = state
        piece = sig[pl.ds(pl.multiple_of(b * BLOCK, BLOCK), BLOCK), :]
        sums = [jnp.sum(in_t[n] * piece, axis=0, keepdims=True) for n in range(poles)]
        return span * state + jnp.concatenate(sums, axis=0)

    state = lax.fori_loop(0, rows // BLOCK, step, jnp.zeros((poles, width), f32), unroll=8)
    pkg[0:poles, :] = state
    pkg[poles : poles + 2, :] = pad[6 + rows : 8 + rows, :]
    pkg[poles + 2 : poles + 4, :] = gate[0:2, :].astype(f32)
    pkg[poles + 4 :, :] = jnp.zeros((pkg.shape[0] - poles - 4, width), f32)


def local_kernel(sig, filt, skip, out, pad):
    rows, width = sig.shape
    pad[0:BLOCK, :] = jnp.zeros((BLOCK, width), jnp.float32)

    def step(b, carry):
        at = pl.ds(pl.multiple_of(b * BLOCK, BLOCK), BLOCK)
        piece = sig[at, :]
        pad[BLOCK : 2 * BLOCK, :] = piece
        for lane in range(width // HD):
            cols = slice(lane * HD, (lane + 1) * HD)
            total = (skip[0:1, cols] + filt[0:1, cols]) * piece[:, cols]
            for k in range(1, BLOCK):
                total = total + filt[k : k + 1, cols] * pad[BLOCK - k : 2 * BLOCK - k, cols]
            out[at, cols] = total
        return carry

    lax.fori_loop(0, rows // BLOCK, step, 0, unroll=2)


def finish_kernel(
    local, blocks, g0, g1, g2, g3, out_t, rate_ref, res_ref, taps, skip, gate, out, pk, st
):
    rows, width = local.shape
    poles = rate_ref.shape[0]
    f32 = jnp.float32
    x = lax.axis_index("x")
    yl = lax.axis_index("yl")
    here = 2 * x + yl
    for d, ref in enumerate((g0, g1, g2, g3)):
        pk[d] = ref[...]
    rate = rate_ref[...]
    segment_decay = jnp.exp(-rate * rows)
    almost_decay = jnp.exp(-rate * (rows - 1))
    t1, t2 = (taps[1:2, :], taps[2:3, :])

    def first_two(package, rim):
        d0 = package[poles + 2 : poles + 3, :] * (t1 * rim[1:2, :] + t2 * rim[0:1, :])
        d1 = package[poles + 3 : poles + 4, :] * (t2 * rim[1:2, :])
        return (d0, d1)

    state = jnp.zeros((poles, width), f32)
    rim = jnp.zeros((2, width), f32)
    for s in range(NX * NYL - 1):
        package = pk[(x - (s >> 1)) & 3, (s & 1) ^ yl]
        d0, d1 = first_two(package, rim)
        full = package[0:poles, :] + segment_decay * d0 + almost_decay * d1
        live = s < here
        state = jnp.where(live, state * segment_decay + full, state)
        rim = jnp.where(live, package[poles : poles + 2, :], rim)
    d0, d1 = first_two(pk[0, 0], rim)
    grow = jnp.exp(rate)
    start = state + d0 + d1 * grow
    before = jnp.sum(res_ref[...] * grow, axis=0, keepdims=True)
    for b in range(rows // BLOCK):
        st[b] = blocks[b] + start * jnp.exp(-rate * (b * BLOCK))
    row = lax.broadcasted_iota(jnp.int32, (BLOCK, width), 0)
    extra = jnp.where(row == 0, skip[...] * d0 - before * d1, 0.0)
    extra = extra + jnp.where(row == 1, skip[...] * d1, 0.0)

    def step(b, carry):
        at = pl.ds(pl.multiple_of(b * BLOCK, BLOCK), BLOCK)
        states = st[b]
        total = local[at, :] + jnp.where(b == 0, extra, 0.0)
        for n in range(poles):
            total = total + out_t[n] * states[n : n + 1, :]
        out[at, :] = (gate[at, :].astype(f32) * total).astype(jnp.bfloat16)
        return carry

    lax.fori_loop(0, rows // BLOCK, step, 0, unroll=8)


def tie(value, *others):
    return lax.optimization_barrier((value,) + others)[0]


def shift(value, axis, count, by):
    return lax.ppermute(value, axis, [(i, (i + by) % count) for i in range(count)])


def per_device(
    residual_in,
    query_rows,
    key_rows,
    value_rows,
    out_weight,
    gate_in,
    gate_out,
    short_taps,
    decay_rates,
    residues,
    skip_gain,
):
    rows, width = residual_in.shape
    half = rows // 2
    bf16, f32 = (jnp.bfloat16, jnp.float32)
    poles = decay_rates.shape[0]
    skip = skip_gain.reshape(1, width)

    packed = local_call(pack_kernel, [struct((rows + half, HD), bf16)] * 4, 4, near=False)(query_rows, key_rows, value_rows)
    came = [None] * 4
    for a in (1, 3, 0, 2):
        came[a] = lax.ppermute(packed[a], ("x", "c"), head_route(a))
    odd_m = jnp.stack([came[1][:rows], came[3][:rows]])
    even_m = jnp.stack([came[0][:rows], came[2][:rows]])
    odd_far = shift(odd_m, "yl", NYL, 1)
    even_far = shift(even_m, "yl", NYL, 1)
    odd_x = shift(odd_m, "c", NC, 1)
    even_x = shift(even_m, "c", NC, 1)
    kv = [pltpu.VMEM((4, rows, HD), bf16)] * 2 + [pltpu.VMEM((10, half, rows), f32)]
    near = local_call(
        near_kernel,
        [struct((4, half, HD), bf16)] + [struct((4, half, HD), f32)] * 3,
        12,
        kv,
        micros=4,
    )(*came, odd_m, even_m, odd_x, even_x)

    k_rows = out_weight.shape[0]
    w_keep, w_send = local_call(
        weight_pick_kernel, [struct((NZ * NYH, k_rows, width), bf16)] * 2, 2
    )(tie(out_weight, near[3]))
    w_recv = shift(w_send, "c", NC, 1)
    out_t, in_t, filt = local_call(
        tables_kernel,
        [struct((poles, BLOCK, width), f32)] * 2 + [struct((BLOCK, width), f32)],
        2,
    )(decay_rates, residues)

    odd_far_x = shift(odd_far, "c", NC, 1)
    even_far_x = shift(tie(even_far, near[3]), "c", NC, 1)
    heads = local_call(
        far_kernel,
        [struct((half, HD), bf16)] * 4,
        12,
        kv + [pltpu.VMEM((4, half, HD), bf16)],
        micros=4,
    )(*near, odd_far, even_far, odd_far_x, even_far_x)
    hm = jnp.stack([heads[0]] + [shift(heads[d], "x", NX, d) for d in range(1, 4)])
    ho = shift(hm, "c", NC, 1)

    part = project(hm, ho, w_keep, w_recv, [4])
    part.update(project(hm, ho, w_keep, w_recv, [3, -3, 2, -2, 1, -1, 0]))

    def join(received, mine):
        return (received.astype(f32) + mine.astype(f32)).astype(bf16)

    def hop(moving, by, across):
        if not across:
            return shift(moving, "z", NZ, by)
        pairs = [
            (z * NYH + y, (z + by) % NZ * NYH + 1 - y) for z in range(NZ) for y in range(NYH)
        ]
        return lax.ppermute(moving, ("z", "yh"), pairs)

    def chain(which, offsets, by):
        moving = part[offsets[0]][which]
        for place, offset in enumerate(offsets):
            if place:
                moving = join(moving, part[offset][which])
            moving = hop(moving, by, which == 0 and abs(offset) == 1)
        return moving

    plus_o = chain(0, [4, 3, 2, 1], 1)
    minus_o = chain(0, [-3, -2, -1], -1)
    own_o = shift(part[0][0], "yh", NYH, 1)
    minus_p = chain(1, [4, -3, -2, -1], -1)
    plus_p = chain(1, [3, 2, 1], 1)

    attended, signal, blocks, package = local_call(
        signal_kernel,
        [
            struct((rows, width), bf16),
            struct((rows, width), f32),
            struct((rows // BLOCK, poles, width), f32),
            struct((poles + 8, width), f32),
        ],
        4,
        [pltpu.VMEM((rows + 8, width), f32)],
        big=[struct((rows, width), bf16)],
    )(part[0][1], plus_p, minus_p, plus_o, minus_o, own_o, residual_in, gate_in, short_taps, decay_rates, in_t)
    pair = jnp.stack([package, shift(package, "yl", NYL, 1)])
    pairs = [pair] + [shift(pair, "x", NX, d) for d in range(1, 4)]
    (local,) = local_call(
        local_kernel,
        [struct((rows, width), f32)],
        2,
        [pltpu.VMEM((2 * BLOCK, width), f32)],
        micros=6,
    )(signal, filt, skip)
    (hyena_out,) = local_call(
        finish_kernel,
        [struct((rows, width), bf16)],
        4,
        [
            pltpu.VMEM((4, 2, poles + 8, width), f32),
            pltpu.VMEM((rows // BLOCK, poles, width), f32),
        ],
        big=[struct((rows, width), bf16)],
    )(local, blocks, *pairs, out_t, decay_rates, residues, short_taps, skip, gate_out)
    return (attended, hyena_out)


def solution(mesh):
    fine = Mesh(
        mesh.devices.reshape(NX, NYL, NZ, NYH, NC), ("x", "yl", "z", "yh", "c")
    ) if hasattr(mesh, "devices") else mesh
    ctx, mp = (("x", "yl"), ("z", "yh", "c"))
    in_specs = (
        P(ctx, mp),
        P(ctx, mp),
        P(ctx, mp),
        P(ctx, mp),
        P(mp, None),
        P(ctx, mp),
        P(ctx, mp),
        P(None, mp),
        P(None, mp),
        P(None, mp),
        P(mp),
    )
    return jax.shard_map(
        per_device,
        mesh=fine,
        in_specs=in_specs,
        out_specs=(P(ctx, mp), P(ctx, mp)),
        check_vma=False,
    )
```
